32 devices in a mesh: gx: 4 (over y, x), gy: 8 (over z, core).
Axes of the slice: x: 2, y: 2, z: 4, core: 2. Of those that a mesh axis runs over, the one named last changes fastest.
Arguments:
- posterior: bfloat16 [8192, 1000], P(('gx', 'gy')), may hold values from -6 to 6
- class_affinity: bfloat16 [8192, 1000], P(('gx', 'gy')), may hold values from 0.049804688 to 20
- band_tiles: bfloat16 [64, 4, 128, 128], P(('gx', 'gy')), may hold values from 9.9658966e-05 to 1
- band_offset: int32 [64, 4], P(('gx', 'gy')), may hold values from -1 to 1
- band_count: int32 [64], P(('gx', 'gy')), may hold values from 1 to 4
- far_tiles: bfloat16 [32, 4, 128, 128], P(('gx', 'gy')), may hold values from 9.9658966e-05 to 1
- far_row: int32 [32, 4], P(('gx', 'gy')), may hold values from 0 to 1
- far_block: int32 [32, 4], P(('gx', 'gy')), may hold values from 0 to 1
Outputs:
- propagated: bfloat16 [8192, 1000], P(('gx', 'gy'))
The draws below stay inside these ranges and needn't reach their ends.
Inputs may be any that keep to these rules, and one draw needn't show every extreme that they name: Near tiles of a slot index at or above band_count of their row block are not part of the graph.
All inputs are finite; a program needn't handle non-finite values.
Results may differ from the reference program's by a relative error of at most 0.002.
Values may be sent and summed in bfloat16 or wider, within the bound.
A program may use at most 64 MiB of HBM per device.

```python
import math
import jax
import jax.numpy as jnp
from jax import lax

CLASSES = 1000
TILE_SIZE = 128
BLOCKS_DEV = 2
SLOTS = 4
BAND_REACH = 1
SWEEPS = 2
ALL_BLOCKS = 64
ALL_NODES = 8192
N_GX = 4
N_GY = 8
DEVICES = 32


def touch_ends(result, own_key, low, top_value):
    longest = result.shape.index(max(result.shape))
    spots = []
    for shift in (0, 1):
        where = [jax.random.randint(jax.random.fold_in(own_key, axis), (), 0, length) for axis, length in enumerate(result.shape)]
        where[longest] = (where[longest] + shift) % result.shape[longest]
        spots.append(tuple(where))
    return result.at[spots[0]].set(low).at[spots[1]].set(top_value)


def block_levels(stream_key, shape, shards, low, largest):
    def one(axis_at, blocks):
        draws = jax.random.uniform(jax.random.fold_in(jax.random.fold_in(stream_key, 6), axis_at), (blocks,), jnp.float32, low / len(shards), largest / len(shards))
        return jnp.repeat(jnp.exp(draws), shape[axis_at] // blocks).reshape((-1,) + (1,) * (len(shape) - axis_at - 1))

    factor_of = one(*shards[0])
    for cut in shards[1:]:
        factor_of = factor_of * one(*cut)
    return factor_of


def scatter_about(own_key, dims, deviation, most, cuts=(), kind=jnp.bfloat16):
    drawn = jax.random.normal(own_key, dims, jnp.float32) * deviation
    if len(cuts) > 0:
        drawn = block_levels(own_key, dims, cuts, -0.22, 0.18) * drawn
    return jnp.clip(drawn, min=-most, max=most).astype(kind)


def setup_inputs(seed: int = 0) -> dict:
    splits = jax.random.split(jax.random.key(seed), 9)
    posterior = scatter_about(splits[0], (ALL_NODES, CLASSES), 1.0, 6.0, ((0, 32),))
    class_affinity = jnp.clip(jnp.exp(math.log(20.0) - 5.9953784 * jax.random.uniform(splits[1], (ALL_NODES, CLASSES), jnp.float32) ** block_levels(splits[1], (ALL_NODES, CLASSES), ((0, 32),), -0.2, 0.2)), 0.049804688, 20.0).astype(jnp.bfloat16)
    band_tiles = jnp.clip(jnp.exp(math.log(1.0) - 9.213757 * jax.random.uniform(splits[2], (ALL_BLOCKS, SLOTS, TILE_SIZE, TILE_SIZE), jnp.float32) ** block_levels(splits[2], (ALL_BLOCKS, SLOTS, TILE_SIZE, TILE_SIZE), ((0, 32),), -0.2, 0.2)), 9.965896606445312e-05, 1.0).astype(jnp.bfloat16)
    band_offset = touch_ends(jax.random.randint(splits[3], (ALL_BLOCKS, SLOTS), 0 - BAND_REACH, BAND_REACH + 1), jax.random.fold_in(splits[3], 1), 0 - BAND_REACH, BAND_REACH).astype(jnp.int32)
    band_count = touch_ends(jax.random.randint(splits[4], (ALL_BLOCKS,), 1, SLOTS + 1), jax.random.fold_in(splits[4], 1), 1, SLOTS).astype(jnp.int32)
    far_tiles = jnp.clip(jnp.exp(math.log(1.0) - 9.213757 * jax.random.uniform(splits[5], (DEVICES, N_GX, TILE_SIZE, TILE_SIZE), jnp.float32) ** block_levels(splits[5], (DEVICES, N_GX, TILE_SIZE, TILE_SIZE), ((0, 32),), -0.2, 0.2)), 9.965896606445312e-05, 1.0).astype(jnp.bfloat16)
    far_row = touch_ends(jax.random.randint(splits[6], (DEVICES, N_GX), 0, BLOCKS_DEV), jax.random.fold_in(splits[6], 1), 0, BLOCKS_DEV - 1).astype(jnp.int32)
    far_block = touch_ends(jax.random.randint(splits[7], (DEVICES, N_GX), 0, BLOCKS_DEV), jax.random.fold_in(splits[7], 1), 0, BLOCKS_DEV - 1).astype(jnp.int32)
    return dict(posterior=posterior, class_affinity=class_affinity, band_tiles=band_tiles, band_offset=band_offset, band_count=band_count, far_tiles=far_tiles, far_row=far_row, far_block=far_block)


propagation_weight = 0.9
epsilon = 1e-06

def normalize(mixed_rows):
    row_scale = lax.rsqrt(lax.optimization_barrier(jnp.mean(mixed_rows * mixed_rows, axis=-1, keepdims=True)) + epsilon)
    return (mixed_rows * row_scale).astype(jnp.bfloat16)

def reference(posterior, class_affinity, band_tiles, band_offset, band_count, far_tiles, far_row, far_block):
    class_count = posterior.shape[1]
    device_count = N_GX * N_GY
    group_blocks = BLOCKS_DEV * N_GY
    slot_ids = jnp.arange(SLOTS, dtype=jnp.int32)
    peer_ids = jnp.arange(N_GX, dtype=jnp.int32)
    block_ids = jnp.arange(BLOCKS_DEV, dtype=jnp.int32)
    current = posterior
    for sweep in range(SWEEPS):
        blocks_all = current.reshape(device_count * BLOCKS_DEV, TILE_SIZE, class_count)

        def one_device(device):
            device = device.astype(jnp.int32)
            outer_index = device // N_GY
            inner_index = device % N_GY
            first_block = device * BLOCKS_DEV
            rows_here = first_block + block_ids
            tile_block = lax.dynamic_slice_in_dim(band_tiles, first_block, BLOCKS_DEV, 0)
            offsets = lax.dynamic_slice_in_dim(band_offset, first_block, BLOCKS_DEV, 0)
            counts = lax.dynamic_slice_in_dim(band_count, first_block, BLOCKS_DEV, 0)
            group_base = outer_index * group_blocks
            columns = (group_base + (rows_here[:, None] - group_base + offsets) % group_blocks).astype(jnp.int32)
            live_mask = (slot_ids[None, :] < counts[:, None]).astype(jnp.float32)
            sources = blocks_all[columns]
            band_sum = jnp.einsum('bsij,bsjc->bic', tile_block.astype(jnp.float32) * live_mask[:, :, None, None], sources.astype(jnp.float32))
            far_block_tiles = far_tiles[device]
            far_rows = far_row[device]
            far_source = far_block[device]
            far_columns = ((peer_ids * N_GY + inner_index) * BLOCKS_DEV + far_source).astype(jnp.int32)
            far_sources = blocks_all[far_columns]
            far_parts = jnp.einsum('qij,qjc->qic', far_block_tiles.astype(jnp.float32), far_sources.astype(jnp.float32))
            owner_table = (far_rows[None, :] == block_ids[:, None]).astype(jnp.float32)
            far_sum = jnp.einsum('bq,qic->bic', owner_table, far_parts)
            combined = (band_sum + far_sum).reshape(BLOCKS_DEV * TILE_SIZE, class_count)
            affinity_rows = lax.dynamic_slice_in_dim(class_affinity, first_block * TILE_SIZE, BLOCKS_DEV * TILE_SIZE, 0)
            mixed_rows = propagation_weight * combined + affinity_rows.astype(jnp.float32)
            return normalize(mixed_rows)
        current = lax.map(one_device, jnp.arange(device_count, dtype=jnp.int32)).reshape(device_count * BLOCKS_DEV * TILE_SIZE, class_count)
    return current
```

```python
import functools

import jax
import jax.numpy as jnp
from jax import lax
from jax.experimental import pallas as pl
from jax.experimental.pallas import tpu as pltpu
from jax.sharding import PartitionSpec as P

SWEEPS = 2
propagation_weight = 0.9
epsilon = 1e-06
MESH = pl.DeviceIdType.MESH


def partner(me, step, peers):
    total = 0
    bit = 1
    while bit < peers:
        here = lax.rem(me // bit, 2)
        total = total + bit * (lax.rem(here + 1, 2) if step & bit else here)
        bit *= 2
    return total


def kernel(
    peers, ring,
    post, aff_hbm, band_hbm, far_hbm, boff, bcnt, frow, fblk,
    out,
    own, exts, stage, arrived, ask, asked, aff, band, far, near_weights, far_weights, acc,
    load_sem, halo_send, halo_recv, far_send, far_recv, ask_send, ask_recv,
):
    me = lax.axis_index("gx")
    spot = lax.axis_index("gy")
    up = lax.rem(spot + 1, ring)
    down = lax.rem(spot + ring - 1, ring)
    blocks, slots, tile, _ = band.shape
    classes = post.shape[0]
    steps = sorted(range(1, peers), key=lambda r: (-bin(r).count("1"), r))
    mates = {r: partner(me, r, peers) for r in range(peers)}

    barrier = pltpu.get_barrier_semaphore()
    for r in steps:
        pl.semaphore_signal(barrier, inc=1, device_id={"gx": mates[r]}, device_id_type=MESH)
    for side in (up, down):
        pl.semaphore_signal(barrier, inc=1, device_id={"gy": side}, device_id_type=MESH)

    def block_of(ref, b):
        return ref.at[:, pl.ds(b * tile, tile)]

    loads = [
        pltpu.make_async_copy(block_of(post, b), target, load_sem.at[3 + 2 * b + k])
        for b in range(blocks)
        for k, target in enumerate((own[0].at[b], exts[0].at[1 + b]))
    ]
    band_load = pltpu.make_async_copy(band_hbm, band, load_sem.at[0])
    far_load = pltpu.make_async_copy(far_hbm, far, load_sem.at[1])
    aff_load = pltpu.make_async_copy(aff_hbm, aff, load_sem.at[2])
    for load in loads + [band_load, far_load, aff_load]:
        load.start()
    for r in steps:
        ask[r] = jnp.full(ask.shape[1:], fblk[0, mates[r]], jnp.int32)
    pl.semaphore_wait(barrier, len(steps) + 2)

    def question(r):
        return pltpu.make_async_remote_copy(
            src_ref=ask.at[r], dst_ref=asked.at[r],
            send_sem=ask_send.at[r], recv_sem=ask_recv.at[r],
            device_id={"gx": mates[r]}, device_id_type=MESH,
        )

    def far_copy(sweep, r):
        return pltpu.make_async_remote_copy(
            src_ref=stage.at[sweep, r], dst_ref=arrived.at[sweep, r],
            send_sem=far_send.at[sweep, r], recv_sem=far_recv.at[sweep, r],
            device_id={"gx": mates[r]}, device_id_type=MESH,
        )

    def halo_copies(sweep, source):
        return [
            pltpu.make_async_remote_copy(
                src_ref=source(blocks - 1), dst_ref=exts[sweep].at[0],
                send_sem=halo_send.at[sweep, 0], recv_sem=halo_recv.at[sweep, 0],
                device_id={"gy": up}, device_id_type=MESH,
            ),
            pltpu.make_async_remote_copy(
                src_ref=source(0), dst_ref=exts[sweep].at[blocks + 1],
                send_sem=halo_send.at[sweep, 1], recv_sem=halo_recv.at[sweep, 1],
                device_id={"gy": down}, device_id_type=MESH,
            ),
        ]

    questions = {r: question(r) for r in steps}
    for r in steps:
        questions[r].start()
    halos = halo_copies(0, lambda b: block_of(post, b))
    for copy in halos:
        copy.start()

    band_load.wait()
    for b in range(blocks):
        for s in range(slots):
            live = jnp.where(s < bcnt[b], 1.0, 0.0).astype(jnp.bfloat16)
            near_weights[b, pl.ds(s * tile, tile), :] = (band[b, s] * live).T
    far_load.wait()
    for r in range(peers):
        weights = far[0, mates[r]].T
        home = frow[0, mates[r]]
        for b in range(blocks):
            mine = jnp.where(home == b, 1.0, 0.0).astype(jnp.bfloat16)
            far_weights[r, :, pl.ds(b * tile, tile)] = weights * mine
    for load in loads:
        load.wait()

    wanted = {}
    for r in steps:
        questions[r].wait()
        wanted[r] = jnp.max(asked[r])
    aff_load.wait()

    cuts = [(c, min(256, classes - c)) for c in range(0, classes, 256)]
    for sweep in range(SWEEPS):
        for r in steps:
            stage[sweep, r] = own[sweep][wanted[r]]
        moves = {r: far_copy(sweep, r) for r in steps}
        for r in steps:
            moves[r].start()
        if sweep > 0:
            halos = halo_copies(sweep, lambda b: own[sweep].at[b])
            for copy in halos:
                copy.start()
        for c, w in cuts:
            acc[pl.ds(c, w), :] = jnp.dot(
                own[sweep][fblk[0, me], pl.ds(c, w), :], far_weights[0],
                preferred_element_type=jnp.float32,
            )
        for copy in halos:
            copy.wait()
        for b in range(blocks):
            lanes = pl.ds(b * tile, tile)
            for c, w in cuts:
                near = jnp.concatenate(
                    [exts[sweep][b + 1 + boff[b, s], pl.ds(c, w), :] for s in range(slots)], axis=1
                )
                acc[pl.ds(c, w), lanes] += jnp.dot(
                    near, near_weights[b], preferred_element_type=jnp.float32
                )
        for at, r in enumerate(steps):
            moves[r].wait()
            if at < len(steps) - 1:
                for c, w in cuts:
                    acc[pl.ds(c, w), :] += jnp.dot(
                        arrived[sweep, r, pl.ds(c, w), :], far_weights[r],
                        preferred_element_type=jnp.float32,
                    )
        r = steps[-1]
        squares = jnp.zeros((1, blocks * tile), jnp.float32)
        for c, w in cuts:
            mixed = acc[pl.ds(c, w), :] + jnp.dot(
                arrived[sweep, r, pl.ds(c, w), :], far_weights[r],
                preferred_element_type=jnp.float32,
            )
            mixed = propagation_weight * mixed + aff[pl.ds(c, w), :].astype(jnp.float32)
            acc[pl.ds(c, w), :] = mixed
            squares += jnp.sum(mixed * mixed, axis=0, keepdims=True)
        scale = lax.rsqrt(squares / classes + epsilon)
        for c, w in cuts:
            value = (acc[pl.ds(c, w), :] * scale).astype(jnp.bfloat16)
            if sweep < SWEEPS - 1:
                for b in range(blocks):
                    part = value[:, b * tile : (b + 1) * tile]
                    own[sweep + 1][b, pl.ds(c, w), :] = part
                    exts[sweep + 1][1 + b, pl.ds(c, w), :] = part
            else:
                out[pl.ds(c, w), :] = value


def local(peers, ring, posterior, affinity, band_tiles, offset, count, far_tiles, far_row, far_block):
    rows, classes = posterior.shape
    blocks, slots, tile, _ = band_tiles.shape
    anywhere = pl.BlockSpec(memory_space=pl.ANY)
    scalars = pl.BlockSpec(memory_space=pltpu.SMEM)
    kind = jnp.bfloat16
    result = pl.pallas_call(
        functools.partial(kernel, peers, ring),
        out_shape=jax.ShapeDtypeStruct((classes, rows), kind),
        in_specs=[anywhere] * 4 + [scalars] * 4,
        out_specs=pl.BlockSpec(memory_space=pltpu.VMEM),
        scratch_shapes=[
            [pltpu.VMEM((blocks, classes, tile), kind)] * SWEEPS,
            [pltpu.VMEM((blocks + 2, classes, tile), kind)] * SWEEPS,
            pltpu.VMEM((SWEEPS, peers, classes, tile), kind),
            pltpu.VMEM((SWEEPS, peers, classes, tile), kind),
            pltpu.VMEM((peers, 8, 128), jnp.int32),
            pltpu.VMEM((peers, 8, 128), jnp.int32),
            pltpu.VMEM((classes, rows), kind),
            pltpu.VMEM(band_tiles.shape, kind),
            pltpu.VMEM(far_tiles.shape, kind),
            pltpu.VMEM((blocks, slots * tile, tile), kind),
            pltpu.VMEM((peers, tile, rows), kind),
            pltpu.VMEM((classes, rows), jnp.float32),
            pltpu.SemaphoreType.DMA((3 + 2 * blocks,)),
            pltpu.SemaphoreType.DMA((SWEEPS, 2)),
            pltpu.SemaphoreType.DMA((SWEEPS, 2)),
            pltpu.SemaphoreType.DMA((SWEEPS, peers)),
            pltpu.SemaphoreType.DMA((SWEEPS, peers)),
            pltpu.SemaphoreType.DMA((peers,)),
            pltpu.SemaphoreType.DMA((peers,)),
        ],
        compiler_params=pltpu.CompilerParams(collective_id=0, has_side_effects=True, vmem_limit_bytes=60 * 2**20),
    )(
        posterior.T, affinity.T, band_tiles, far_tiles,
        offset, count, far_row, far_block,
    )
    return result.T


def solution(mesh):
    spread = ("gx", "gy")
    in_specs = (
        P(spread, None), P(spread, None), P(spread, None, None, None), P(spread, None),
        P(spread), P(spread, None, None, None), P(spread, None), P(spread, None),
    )

    def run(posterior, affinity, band_tiles, offset, count, far_tiles, far_row, far_block):
        return local(
            mesh.shape["gx"], mesh.shape["gy"],
            posterior, affinity, band_tiles, offset, count, far_tiles, far_row, far_block,
        )

    return jax.shard_map(run, mesh=mesh, in_specs=in_specs, out_specs=P(spread, None), check_vma=False)
```

```python
import functools

import jax
import jax.numpy as jnp
from jax import lax
from jax.experimental import pallas as pl
from jax.experimental.pallas import tpu as pltpu
from jax.sharding import PartitionSpec as P

SWEEPS = 2
propagation_weight = 0.9
epsilon = 1e-06
FIRST = 128
PIECES = 3
BRIDGE = 1
MESH = pl.DeviceIdType.MESH


def partner(me, step, peers):
    total = 0
    bit = 1
    while bit < peers:
        here = lax.rem(me // bit, 2)
        total = total + bit * (lax.rem(here + 1, 2) if step & bit else here)
        bit *= 2
    return total


def chunks_of(classes):
    first = min(FIRST, classes)
    cuts = [(0, first)]
    rest = classes - first
    if rest:
        size = -(-rest // (PIECES * 16)) * 16
        cuts += [(c, min(size, classes - c)) for c in range(first, classes, size)]
    return cuts


def kernel(
    peers, ring, cuts,
    post, aff_hbm, band_hbm, far_hbm, boff_hbm, bcnt_hbm, frow_hbm, fblk_hbm,
    out, scale_out,
    own, exts, early, stage, arrived, ask, asked, aff, band, far, near_weights, far_weights, acc,
    boff, bcnt, frow, fblk, scales, far_scale_out, far_scale_in,
    load_sem, halo_send, halo_recv, far_send, far_recv, ask_send, ask_recv, scale_send, scale_recv,
):
    me = lax.axis_index("gx")
    spot = lax.axis_index("gy")
    up = lax.rem(spot + 1, ring)
    down = lax.rem(spot + ring - 1, ring)
    blocks, slots, tile, _ = band.shape
    classes = post.shape[0]
    steps = sorted(range(1, peers), key=lambda r: (-bin(r).count("1"), r))
    mates = {r: partner(me, r, peers) for r in range(peers)}

    barrier = pltpu.get_barrier_semaphore()
    for side in (up, down):
        pl.semaphore_signal(barrier, inc=1, device_id={"gy": side}, device_id_type=MESH)
    for r in steps:
        pl.semaphore_signal(barrier, inc=1, device_id={"gx": mates[r]}, device_id_type=MESH)

    pending = []

    def load(source, target):
        copy = pltpu.make_async_copy(source, target, load_sem.at[len(pending)])
        copy.start()
        pending.append(copy)
        return copy

    words = [
        load(source, target)
        for source, target in ((fblk_hbm, fblk), (frow_hbm, frow), (bcnt_hbm, bcnt), (boff_hbm, boff))
    ]
    mine = [load(post.at[:, pl.ds(b * tile, tile)], own[0].at[b]) for b in range(blocks)]
    band_load = load(band_hbm, band)
    far_load = load(far_hbm, far)
    aff_load = load(aff_hbm, aff)
    for copy in words:
        copy.wait()
    for r in steps:
        ask[r] = jnp.full(ask.shape[1:], fblk[0, mates[r]], jnp.int32)
    for copy in mine:
        copy.wait()
    for k, (c, w) in enumerate(cuts):
        for b in range(blocks):
            exts[0][k][1 + b] = own[0][b, pl.ds(c, w), :]
    pl.semaphore_wait(barrier, len(steps) + 2)

    def to_mate(r, source, target, send, recv):
        return pltpu.make_async_remote_copy(
            src_ref=source, dst_ref=target, send_sem=send, recv_sem=recv,
            device_id={"gx": mates[r]}, device_id_type=MESH,
        )

    def to_sides(first, last, before, after, send, recv):
        return [
            pltpu.make_async_remote_copy(
                src_ref=source, dst_ref=target, send_sem=send.at[i], recv_sem=recv.at[i],
                device_id={"gy": side}, device_id_type=MESH,
            )
            for i, (source, target, side) in enumerate(((last, before, up), (first, after, down)))
        ]

    def send_halo(sweep, k):
        c, w = cuts[k]
        copies = to_sides(
            own[sweep].at[0, pl.ds(c, w)], own[sweep].at[blocks - 1, pl.ds(c, w)],
            exts[sweep][k].at[0], exts[sweep][k].at[blocks + 1],
            halo_send.at[sweep, k], halo_recv.at[sweep, k],
        )
        for copy in copies:
            copy.start()
        return copies

    def send_far(sweep, k):
        c, w = cuts[k]
        for r in steps:
            stage[sweep, r, pl.ds(c, w), :] = own[sweep][wanted[r], pl.ds(c, w), :]
        copies = [
            to_mate(
                r, stage.at[sweep, r, pl.ds(c, w)], arrived.at[sweep, r, pl.ds(c, w)],
                far_send.at[sweep, k, r], far_recv.at[sweep, k, r],
            )
            for r in steps
        ]
        for copy in copies:
            copy.start()
        return copies

    questions = {r: to_mate(r, ask.at[r], asked.at[r], ask_send.at[r], ask_recv.at[r]) for r in steps}
    for r in steps:
        questions[r].start()
    c, w = cuts[0]
    far_moves, halo_moves = {}, {}
    far_moves[0, 0] = [
        to_mate(
            r, own[0].at[:, pl.ds(c, w)], early.at[r], far_send.at[0, 0, r], far_recv.at[0, 0, r]
        )
        for r in steps
    ]
    for copy in far_moves[0, 0]:
        copy.start()
    for k in range(len(cuts)):
        halo_moves[0, k] = send_halo(0, k)

    wanted = {}
    for r in steps:
        questions[r].wait()
        wanted[r] = jnp.max(asked[r])
    for k in range(1, len(cuts)):
        far_moves[0, k] = send_far(0, k)

    def weights():
        for b in range(blocks):
            for s in range(slots):
                live = jnp.where(s < bcnt[b], 1.0, 0.0)
                part = band[b, s].astype(jnp.float32) * live
                near_weights[b, pl.ds(s * tile, tile), :] = part.astype(jnp.bfloat16).T
        for r in range(peers):
            part = far[0, mates[r]].T
            home = frow[0, mates[r]]
            for b in range(blocks):
                chosen = jnp.where(home == b, 1.0, 0.0).astype(jnp.bfloat16)
                far_weights[pl.ds(r * tile, tile), pl.ds(b * tile, tile)] = part * chosen

    band_load.wait()
    far_load.wait()
    weights()
    aff_load.wait()

    def times(value, row):
        return (value.astype(jnp.float32) * row[0:1, :]).astype(jnp.bfloat16)

    def keep(sweep, k, value):
        c, w = cuts[k]
        for b in range(blocks):
            part = value[:, b * tile : (b + 1) * tile]
            own[sweep][b, pl.ds(c, w), :] = part
            exts[sweep][k][1 + b] = part

    scale_moves = {}
    for sweep in range(SWEEPS):
        squares = jnp.zeros((1, blocks * tile), jnp.float32)
        for k, (c, w) in enumerate(cuts):
            rows = pl.ds(c, w)
            raw = sweep > 0 and k < BRIDGE
            if raw and k == 0:
                for copy in scale_moves[sweep]:
                    copy.wait()
            for copy in halo_moves[sweep, k]:
                copy.wait_recv() if raw else copy.wait()
            if raw:
                for e in (0, blocks + 1):
                    exts[sweep][k][e] = times(exts[sweep][k][e], scales[e])
            near = [
                jnp.dot(
                    jnp.concatenate(
                        [exts[sweep][k][b + 1 + boff[b, s]] for s in range(slots)], axis=1
                    ),
                    near_weights[b], preferred_element_type=jnp.float32,
                )
                for b in range(blocks)
            ]
            for copy in far_moves[sweep, k]:
                copy.wait()
            parts = [own[sweep][fblk[0, me], rows, :]]
            for r in range(1, peers):
                if sweep == 0 and k == 0:
                    parts.append(early[r, fblk[0, mates[r]]])
                elif raw:
                    parts.append(times(arrived[sweep, r, rows, :], far_scale_in[r]))
                else:
                    parts.append(arrived[sweep, r, rows, :])
            mixed = jnp.dot(
                jnp.concatenate(parts, axis=1), far_weights[...],
                preferred_element_type=jnp.float32,
            )
            mixed = mixed + jnp.concatenate(near, axis=1)
            mixed = propagation_weight * mixed + aff[rows, :].astype(jnp.float32)
            squares += jnp.sum(mixed * mixed, axis=0, keepdims=True)
            if sweep < SWEEPS - 1:
                acc[rows, :] = mixed
                if k < BRIDGE:
                    keep(sweep + 1, k, mixed.astype(jnp.bfloat16))
                    far_moves[sweep + 1, k] = send_far(sweep + 1, k)
                    halo_moves[sweep + 1, k] = send_halo(sweep + 1, k)
            else:
                out[rows, :] = mixed
        scale = lax.rsqrt(squares / classes + epsilon)
        if sweep == SWEEPS - 1:
            scale_out[...] = jnp.broadcast_to(scale, scale_out.shape)
            continue
        for b in range(blocks):
            scales[1 + b] = jnp.broadcast_to(scale[:, b * tile : (b + 1) * tile], (8, tile))
        for r in steps:
            row = scales[1]
            for b in range(1, blocks):
                row = jnp.where(wanted[r] == b, scales[1 + b], row)
            far_scale_out[r] = row
        scale_moves[sweep + 1] = [
            to_mate(r, far_scale_out.at[r], far_scale_in.at[r], scale_send.at[r], scale_recv.at[r])
            for r in steps
        ] + to_sides(
            scales.at[1], scales.at[blocks], scales.at[0], scales.at[blocks + 1],
            scale_send.at[pl.ds(peers, 2)], scale_recv.at[pl.ds(peers, 2)],
        )
        for copy in scale_moves[sweep + 1]:
            copy.start()
        for k, (c, w) in enumerate(cuts):
            value = (acc[pl.ds(c, w), :] * scale).astype(jnp.bfloat16)
            if k >= BRIDGE:
                keep(sweep + 1, k, value)
                far_moves[sweep + 1, k] = send_far(sweep + 1, k)
                halo_moves[sweep + 1, k] = send_halo(sweep + 1, k)
        for k, (c, w) in enumerate(cuts[:BRIDGE]):
            value = (acc[pl.ds(c, w), :] * scale).astype(jnp.bfloat16)
            for copy in halo_moves[sweep + 1, k]:
                copy.wait_send()
            keep(sweep + 1, k, value)


def local(peers, ring, posterior, affinity, band_tiles, offset, count, far_tiles, far_row, far_block):
    rows, classes = posterior.shape
    blocks, slots, tile, _ = band_tiles.shape
    stored = pl.BlockSpec(memory_space=pltpu.HBM)
    kind = jnp.bfloat16
    cuts = chunks_of(classes)
    pieces = len(cuts)
    scratch = [
        [pltpu.VMEM((blocks, classes, tile), kind)] * SWEEPS,
        [[pltpu.VMEM((blocks + 2, w, tile), kind) for _, w in cuts] for _ in range(SWEEPS)],
        pltpu.VMEM((peers, blocks, cuts[0][1], tile), kind),
        pltpu.VMEM((SWEEPS, peers, classes, tile), kind),
        pltpu.VMEM((SWEEPS, peers, classes, tile), kind),
        pltpu.VMEM((peers, 8, 128), jnp.int32),
        pltpu.VMEM((peers, 8, 128), jnp.int32),
        pltpu.VMEM((classes, rows), kind),
        pltpu.VMEM(band_tiles.shape, kind),
        pltpu.VMEM(far_tiles.shape, kind),
        pltpu.VMEM((blocks, slots * tile, tile), kind),
        pltpu.VMEM((peers * tile, rows), kind),
        pltpu.VMEM((classes, rows), jnp.float32),
        pltpu.SMEM(offset.shape, jnp.int32),
        pltpu.SMEM(count.shape, jnp.int32),
        pltpu.SMEM(far_row.shape, jnp.int32),
        pltpu.SMEM(far_block.shape, jnp.int32),
        pltpu.VMEM((blocks + 2, 8, tile), jnp.float32),
        pltpu.VMEM((peers, 8, tile), jnp.float32),
        pltpu.VMEM((peers, 8, tile), jnp.float32),
        pltpu.SemaphoreType.DMA((7 + blocks,)),
        pltpu.SemaphoreType.DMA((SWEEPS, pieces, 2)),
        pltpu.SemaphoreType.DMA((SWEEPS, pieces, 2)),
        pltpu.SemaphoreType.DMA((SWEEPS, pieces, peers)),
        pltpu.SemaphoreType.DMA((SWEEPS, pieces, peers)),
        pltpu.SemaphoreType.DMA((peers,)),
        pltpu.SemaphoreType.DMA((peers,)),
        pltpu.SemaphoreType.DMA((peers + 2,)),
        pltpu.SemaphoreType.DMA((peers + 2,)),
    ]
    mixed, scale = pl.pallas_call(
        functools.partial(kernel, peers, ring, cuts),
        out_shape=(
            jax.ShapeDtypeStruct((classes, rows), jnp.float32),
            jax.ShapeDtypeStruct((8, rows), jnp.float32),
        ),
        in_specs=[stored] * 8,
        out_specs=(pl.BlockSpec(memory_space=pltpu.VMEM),) * 2,
        scratch_shapes=scratch,
        compiler_params=pltpu.CompilerParams(
            collective_id=0, has_side_effects=True, vmem_limit_bytes=60 * 2**20
        ),
    )(
        posterior.T, affinity.T, band_tiles, far_tiles,
        offset, count, far_row, far_block,
    )
    return (mixed * scale[0:1, :]).astype(kind).T


def solution(mesh):
    spread = ("gx", "gy")
    in_specs = (
        P(spread, None), P(spread, None), P(spread, None, None, None), P(spread, None),
        P(spread), P(spread, None, None, None), P(spread, None), P(spread, None),
    )

    def run(posterior, affinity, band_tiles, offset, count, far_tiles, far_row, far_block):
        return local(
            mesh.shape["gx"], mesh.shape["gy"],
            posterior, affinity, band_tiles, offset, count, far_tiles, far_row, far_block,
        )

    return jax.shard_map(run, mesh=mesh, in_specs=in_specs, out_specs=P(spread, None), check_vma=False)
```

```python
import functools

import jax
import jax.numpy as jnp
from jax import lax
from jax.experimental import pallas as pl
from jax.experimental.pallas import tpu as pltpu
from jax.sharding import PartitionSpec as P

SWEEPS = 2
propagation_weight = 0.9
epsilon = 1e-06
FIRST = 128
PIECES = 3
BRIDGE = 1
MESH = pl.DeviceIdType.MESH


def partner(me, step, peers):
    total = 0
    bit = 1
    while bit < peers:
        here = lax.rem(me // bit, 2)
        total = total + bit * (lax.rem(here + 1, 2) if step & bit else here)
        bit *= 2
    return total


def chunks_of(classes):
    first = min(FIRST, classes)
    cuts = [(0, first)]
    rest = classes - first
    if rest:
        size = -(-rest // (PIECES * 16)) * 16
        cuts += [(c, min(size, classes - c)) for c in range(first, classes, size)]
    return cuts


def kernel(
    peers, ring, cuts,
    post, aff_hbm, band_hbm, far_hbm, boff_hbm, bcnt_hbm, frow_hbm, fblk_hbm,
    out,
    own, exts, early, stage, arrived, ask, asked, aff, band, far, near_weights, far_weights, acc,
    boff, bcnt, frow, fblk, scales, far_scale_out, far_scale_in,
    load_sem, halo_send, halo_recv, far_send, far_recv, ask_send, ask_recv, scale_send, scale_recv,
):
    me = lax.axis_index("gx")
    spot = lax.axis_index("gy")
    up = lax.rem(spot + 1, ring)
    down = lax.rem(spot + ring - 1, ring)
    blocks, slots, tile, _ = band.shape
    classes = post.shape[0]
    steps = sorted(range(1, peers), key=lambda r: (-bin(r).count("1"), r))
    mates = {r: partner(me, r, peers) for r in range(peers)}

    barrier = pltpu.get_barrier_semaphore()
    for side in (up, down):
        pl.semaphore_signal(barrier, inc=1, device_id={"gy": side}, device_id_type=MESH)
    for r in steps:
        pl.semaphore_signal(barrier, inc=1, device_id={"gx": mates[r]}, device_id_type=MESH)

    pending = []

    def load(source, target):
        copy = pltpu.make_async_copy(source, target, load_sem.at[len(pending)])
        copy.start()
        pending.append(copy)
        return copy

    words = [
        load(source, target)
        for source, target in ((fblk_hbm, fblk), (frow_hbm, frow), (bcnt_hbm, bcnt), (boff_hbm, boff))
    ]
    mine = [load(post.at[:, pl.ds(b * tile, tile)], own[0].at[b]) for b in range(blocks)]
    band_load = load(band_hbm, band)
    far_load = load(far_hbm, far)
    aff_load = load(aff_hbm, aff)
    for copy in words:
        copy.wait()
    for r in steps:
        ask[r] = jnp.full(ask.shape[1:], fblk[0, mates[r]], jnp.int32)
    for copy in mine:
        copy.wait()
    for k, (c, w) in enumerate(cuts):
        for b in range(blocks):
            exts[0][k][1 + b] = own[0][b, pl.ds(c, w), :]
    pl.semaphore_wait(barrier, len(steps) + 2)

    def to_mate(r, source, target, send, recv):
        return pltpu.make_async_remote_copy(
            src_ref=source, dst_ref=target, send_sem=send, recv_sem=recv,
            device_id={"gx": mates[r]}, device_id_type=MESH,
        )

    def to_sides(first, last, before, after, send, recv):
        return [
            pltpu.make_async_remote_copy(
                src_ref=source, dst_ref=target, send_sem=send.at[i], recv_sem=recv.at[i],
                device_id={"gy": side}, device_id_type=MESH,
            )
            for i, (source, target, side) in enumerate(((last, before, up), (first, after, down)))
        ]

    def send_halo(sweep, k):
        c, w = cuts[k]
        copies = to_sides(
            own[sweep].at[0, pl.ds(c, w)], own[sweep].at[blocks - 1, pl.ds(c, w)],
            exts[sweep][k].at[0], exts[sweep][k].at[blocks + 1],
            halo_send.at[sweep, k], halo_recv.at[sweep, k],
        )
        for copy in copies:
            copy.start()
        return copies

    def send_far(sweep, k):
        c, w = cuts[k]
        for r in steps:
            stage[sweep, r, pl.ds(c, w), :] = own[sweep][wanted[r], pl.ds(c, w), :]
        copies = [
            to_mate(
                r, stage.at[sweep, r, pl.ds(c, w)], arrived.at[sweep, r, pl.ds(c, w)],
                far_send.at[sweep, k, r], far_recv.at[sweep, k, r],
            )
            for r in steps
        ]
        for copy in copies:
            copy.start()
        return copies

    questions = {r: to_mate(r, ask.at[r], asked.at[r], ask_send.at[r], ask_recv.at[r]) for r in steps}
    for r in steps:
        questions[r].start()
    c, w = cuts[0]
    far_moves, halo_moves = {}, {}
    far_moves[0, 0] = [
        to_mate(
            r, own[0].at[:, pl.ds(c, w)], early.at[r], far_send.at[0, 0, r], far_recv.at[0, 0, r]
        )
        for r in steps
    ]
    for copy in far_moves[0, 0]:
        copy.start()
    for k in range(len(cuts)):
        halo_moves[0, k] = send_halo(0, k)

    wanted = {}
    for r in steps:
        questions[r].wait()
        wanted[r] = jnp.max(asked[r])
    for k in range(1, len(cuts)):
        far_moves[0, k] = send_far(0, k)

    def weights():
        for b in range(blocks):
            for s in range(slots):
                live = jnp.where(s < bcnt[b], 1.0, 0.0)
                part = band[b, s].astype(jnp.float32) * live
                near_weights[b, pl.ds(s * tile, tile), :] = part.astype(jnp.bfloat16).T
        for r in range(peers):
            part = far[0, mates[r]].T
            home = frow[0, mates[r]]
            for b in range(blocks):
                chosen = jnp.where(home == b, 1.0, 0.0).astype(jnp.bfloat16)
                far_weights[pl.ds(r * tile, tile), pl.ds(b * tile, tile)] = part * chosen

    band_load.wait()
    far_load.wait()
    weights()
    aff_load.wait()

    def times(value, row):
        return (value.astype(jnp.float32) * row[0:1, :]).astype(jnp.bfloat16)

    def keep(sweep, k, value):
        c, w = cuts[k]
        for b in range(blocks):
            part = value[:, b * tile : (b + 1) * tile]
            own[sweep][b, pl.ds(c, w), :] = part
            exts[sweep][k][1 + b] = part

    scale_moves = {}
    for sweep in range(SWEEPS):
        squares = jnp.zeros((1, blocks * tile), jnp.float32)
        for k, (c, w) in enumerate(cuts):
            rows = pl.ds(c, w)
            raw = sweep > 0 and k < BRIDGE
            if raw and k == 0:
                for copy in scale_moves[sweep]:
                    copy.wait()
            for copy in halo_moves[sweep, k]:
                copy.wait_recv() if raw else copy.wait()
            if raw:
                for e in (0, blocks + 1):
                    exts[sweep][k][e] = times(exts[sweep][k][e], scales[e])
            near = [
                jnp.dot(
                    jnp.concatenate(
                        [exts[sweep][k][b + 1 + boff[b, s]] for s in range(slots)], axis=1
                    ),
                    near_weights[b], preferred_element_type=jnp.float32,
                )
                for b in range(blocks)
            ]
            for copy in far_moves[sweep, k]:
                copy.wait()
            parts = [own[sweep][fblk[0, me], rows, :]]
            for r in range(1, peers):
                if sweep == 0 and k == 0:
                    parts.append(early[r, fblk[0, mates[r]]])
                elif raw:
                    parts.append(times(arrived[sweep, r, rows, :], far_scale_in[r]))
                else:
                    parts.append(arrived[sweep, r, rows, :])
            mixed = jnp.dot(
                jnp.concatenate(parts, axis=1), far_weights[...],
                preferred_element_type=jnp.float32,
            )
            mixed = mixed + jnp.concatenate(near, axis=1)
            mixed = propagation_weight * mixed + aff[rows, :].astype(jnp.float32)
            squares += jnp.sum(mixed * mixed, axis=0, keepdims=True)
            if sweep < SWEEPS - 1:
                acc[rows, :] = mixed
                if k < BRIDGE:
                    keep(sweep + 1, k, mixed.astype(jnp.bfloat16))
                    far_moves[sweep + 1, k] = send_far(sweep + 1, k)
                    halo_moves[sweep + 1, k] = send_halo(sweep + 1, k)
            else:
                acc[rows, :] = mixed
        scale = lax.rsqrt(squares / classes + epsilon)
        if sweep == SWEEPS - 1:
            for c, w in cuts:
                out[pl.ds(c, w), :] = (acc[pl.ds(c, w), :] * scale).astype(jnp.bfloat16)
            continue
        for b in range(blocks):
            scales[1 + b] = jnp.broadcast_to(scale[:, b * tile : (b + 1) * tile], (8, tile))
        for r in steps:
            row = scales[1]
            for b in range(1, blocks):
                row = jnp.where(wanted[r] == b, scales[1 + b], row)
            far_scale_out[r] = row
        scale_moves[sweep + 1] = [
            to_mate(r, far_scale_out.at[r], far_scale_in.at[r], scale_send.at[r], scale_recv.at[r])
            for r in steps
        ] + to_sides(
            scales.at[1], scales.at[blocks], scales.at[0], scales.at[blocks + 1],
            scale_send.at[pl.ds(peers, 2)], scale_recv.at[pl.ds(peers, 2)],
        )
        for copy in scale_moves[sweep + 1]:
            copy.start()
        for k, (c, w) in enumerate(cuts):
            value = (acc[pl.ds(c, w), :] * scale).astype(jnp.bfloat16)
            if k >= BRIDGE:
                keep(sweep + 1, k, value)
                far_moves[sweep + 1, k] = send_far(sweep + 1, k)
                halo_moves[sweep + 1, k] = send_halo(sweep + 1, k)
        for k, (c, w) in enumerate(cuts[:BRIDGE]):
            value = (acc[pl.ds(c, w), :] * scale).astype(jnp.bfloat16)
            for copy in halo_moves[sweep + 1, k]:
                copy.wait_send()
            keep(sweep + 1, k, value)


def local(peers, ring, posterior, affinity, band_tiles, offset, count, far_tiles, far_row, far_block):
    rows, classes = posterior.shape
    blocks, slots, tile, _ = band_tiles.shape
    stored = pl.BlockSpec(memory_space=pltpu.HBM)
    kind = jnp.bfloat16
    cuts = chunks_of(classes)
    pieces = len(cuts)
    scratch = [
        [pltpu.VMEM((blocks, classes, tile), kind)] * SWEEPS,
        [[pltpu.VMEM((blocks + 2, w, tile), kind) for _, w in cuts] for _ in range(SWEEPS)],
        pltpu.VMEM((peers, blocks, cuts[0][1], tile), kind),
        pltpu.VMEM((SWEEPS, peers, classes, tile), kind),
        pltpu.VMEM((SWEEPS, peers, classes, tile), kind),
        pltpu.VMEM((peers, 8, 128), jnp.int32),
        pltpu.VMEM((peers, 8, 128), jnp.int32),
        pltpu.VMEM((classes, rows), kind),
        pltpu.VMEM(band_tiles.shape, kind),
        pltpu.VMEM(far_tiles.shape, kind),
        pltpu.VMEM((blocks, slots * tile, tile), kind),
        pltpu.VMEM((peers * tile, rows), kind),
        pltpu.VMEM((classes, rows), jnp.float32),
        pltpu.SMEM(offset.shape, jnp.int32),
        pltpu.SMEM(count.shape, jnp.int32),
        pltpu.SMEM(far_row.shape, jnp.int32),
        pltpu.SMEM(far_block.shape, jnp.int32),
        pltpu.VMEM((blocks + 2, 8, tile), jnp.float32),
        pltpu.VMEM((peers, 8, tile), jnp.float32),
        pltpu.VMEM((peers, 8, tile), jnp.float32),
        pltpu.SemaphoreType.DMA((7 + blocks,)),
        pltpu.SemaphoreType.DMA((SWEEPS, pieces, 2)),
        pltpu.SemaphoreType.DMA((SWEEPS, pieces, 2)),
        pltpu.SemaphoreType.DMA((SWEEPS, pieces, peers)),
        pltpu.SemaphoreType.DMA((SWEEPS, pieces, peers)),
        pltpu.SemaphoreType.DMA((peers,)),
        pltpu.SemaphoreType.DMA((peers,)),
        pltpu.SemaphoreType.DMA((peers + 2,)),
        pltpu.SemaphoreType.DMA((peers + 2,)),
    ]
    held = min(8 * rows * classes * (3 + 2 * peers) + 20 * 2**20, 60 * 2**20)
    result = pl.pallas_call(
        functools.partial(kernel, peers, ring, cuts),
        out_shape=jax.ShapeDtypeStruct((classes, rows), kind),
        in_specs=[stored] * 8,
        out_specs=pl.BlockSpec(memory_space=pltpu.VMEM),
        scratch_shapes=scratch,
        compiler_params=pltpu.CompilerParams(
            collective_id=0, has_side_effects=True, vmem_limit_bytes=held
        ),
    )(
        *[
            pltpu.with_memory_space_constraint(value, pltpu.HBM)
            for value in (
                posterior.T, affinity.T, band_tiles, far_tiles, offset, count, far_row, far_block
            )
        ]
    )
    return result.T


def solution(mesh):
    spread = ("gx", "gy")
    in_specs = (
        P(spread, None), P(spread, None), P(spread, None, None, None), P(spread, None),
        P(spread), P(spread, None, None, None), P(spread, None), P(spread, None),
    )

    def run(posterior, affinity, band_tiles, offset, count, far_tiles, far_row, far_block):
        return local(
            mesh.shape["gx"], mesh.shape["gy"],
            posterior, affinity, band_tiles, offset, count, far_tiles, far_row, far_block,
        )

    return jax.shard_map(run, mesh=mesh, in_specs=in_specs, out_specs=P(spread, None), check_vma=False)
```
